256 devices in a mesh: group: 16 (over y_lo, x, core), narrow: 16 (over y_hi, z).
Axes of the slice: x: 4, y: 4 (y_hi: 2, y_lo: 2; y = y_hi * 2 + y_lo), z: 8, core: 2. Of those that a mesh axis runs over, the one named last changes fastest.
Arguments:
- patches: bfloat16 [4096, 3675], P(('group', 'narrow')), may hold values from -8 to 8
- counts: int32 [4096], P(('group', 'narrow')), may hold values from 1 to 49
- weights: float32 [49], replicated, may hold values from 0.3 to 3
- probes: float32 [4096, 16], P(('group', 'narrow')), may hold values from -6 to 6
- plan: int32 [4, 16], replicated, may hold values from 0 to 15, as said below
Outputs:
- product: float32 [4096, 16], P(('group', 'narrow'))
The draws below stay inside these ranges and needn't reach their ends.
Inputs may be any that keep to these rules, and one draw needn't show every extreme that they name: Each row pairs the 16 blocks: plan[m, plan[m, b]] = b and plan[m, b] != b.
All inputs are finite; a program needn't handle non-finite values.
Results may differ from the reference program's by a relative error of at most 0.008.
Values may be sent and summed in bfloat16 or wider, within the bound.
A program may use at most 64 MiB of HBM per device.

```python
import math
import jax
import jax.numpy as jnp
from jax import lax

P_SIZE = 49
PV = 75
NPROBE = 16
MEET = 4
IMG_DEV = 16
NB = 256
NIMG = 4096
N_GROUP = 16
N_NARROW = 16


def draw_patches(key, part):
    first, second, third = jax.random.split(key, 3)
    levels = jax.random.normal(first, (NIMG, P_SIZE, 8), jnp.float32)
    noise = jax.random.normal(third, (NIMG, P_SIZE, PV), jnp.float32)
    scales = jnp.exp(jax.random.uniform(second, (NIMG, P_SIZE, 1), jnp.float32, 0.0, jnp.log(2.1)))
    member = jnp.arange(PV, dtype=jnp.int32) * 8 // PV
    spread = jnp.take(levels * scales, member, axis=2)
    values = spread + 0.3 * noise
    return jnp.clip(values, -8.0, 8.0).reshape(NIMG, P_SIZE * PV).astype(jnp.bfloat16)


def draw_plan(key, part):
    rows = []
    for meeting in range(MEET):
        order = jax.random.permutation(jax.random.fold_in(key, meeting + 11), N_GROUP).astype(jnp.int32)
        left = order[0::2]
        right = order[1::2]
        partner = jnp.zeros((N_GROUP,), jnp.int32).at[left].set(right).at[right].set(left)
        rows.append(partner)
    return jnp.stack(rows, axis=0)


def plant(values, key, low, high):
    longest = values.shape.index(max(values.shape))
    spots = []
    for shift in (0, 1):
        where = [jax.random.randint(jax.random.fold_in(key, axis), (), 0, length) for axis, length in enumerate(values.shape)]
        where[longest] = (where[longest] + shift) % values.shape[longest]
        spots.append(tuple(where))
    return values.at[spots[0]].set(low).at[spots[1]].set(high)


def block_scale(own_key, shape, cuts, low, top_value):
    def one(dim, parts):
        steps = jax.random.uniform(jax.random.fold_in(jax.random.fold_in(own_key, 6), dim), (parts,), jnp.float32, low / len(cuts), top_value / len(cuts))
        return jnp.repeat(jnp.exp(steps), shape[dim] // parts).reshape((-1,) + (1,) * (len(shape) - dim - 1))

    level = one(*cuts[0])
    for cut in cuts[1:]:
        level = level * one(*cut)
    return level


def normal_values(rng, shape, width, reach, cuts=(), kind=jnp.bfloat16):
    values = jax.random.normal(rng, shape, jnp.float32) * width
    if len(cuts) > 0:
        values = block_scale(rng, shape, cuts, -0.22, 0.18) * values
    return jnp.clip(values, min=-reach, max=reach).astype(kind)


def setup_inputs(seed: int = 0) -> dict:
    key_list = jax.random.split(jax.random.key(seed), 6)
    return {
        "patches": draw_patches(jax.random.fold_in(key_list[5], 71), 0),
        "counts": plant(jax.random.randint(key_list[1], (NIMG,), 1, P_SIZE + 1), jax.random.fold_in(key_list[1], 1), 1, P_SIZE).astype(jnp.int32),
        "weights": jnp.clip(jnp.exp(jax.random.uniform(key_list[2], (P_SIZE,), jnp.float32, math.log(0.3), math.log(3.0))), 0.3, 3.0),
        "probes": normal_values(key_list[3], (NIMG, NPROBE), 1.0, 6.0, ((0, 256),), jnp.float32),
        "plan": draw_plan(jax.random.fold_in(key_list[5], 71), 0),
    }


def kernel_tile(rows_x, cols_x):
    inner = lax.dot_general(rows_x, cols_x, (((1,), (1,)), ((), ())), preferred_element_type=jnp.float32)
    rows_f = rows_x.astype(jnp.float32)
    cols_f = cols_x.astype(jnp.float32)
    rows_n = jnp.sum(rows_f * rows_f, axis=1)
    cols_n = jnp.sum(cols_f * cols_f, axis=1)
    return jnp.exp((2.0 * inner - rows_n[:, None] - cols_n[None, :]) / (2.0 * PV)).astype(jnp.bfloat16)


def reference(patches, counts, weights, probes, plan):
    span = IMG_DEV * P_SIZE
    every_x = patches.reshape(N_GROUP, NB * P_SIZE, PV)
    valid = (jnp.arange(P_SIZE, dtype=jnp.int32)[None, :] < counts[:, None]).astype(jnp.float32)
    alpha = weights[None, :] * valid / counts[:, None].astype(jnp.float32)
    every_u = (alpha[:, :, None] * probes[:, None, :]).astype(jnp.bfloat16).reshape(N_GROUP, NB * P_SIZE, NPROBE)
    every_a = alpha.reshape(N_GROUP, NB * P_SIZE)

    def one_group(block):
        rows_x = lax.dynamic_index_in_dim(every_x, block, 0, keepdims=False)
        rows_a = lax.dynamic_index_in_dim(every_a, block, 0, keepdims=False)
        total = jnp.zeros((NB * P_SIZE, NPROBE), jnp.float32)
        for meeting in range(MEET):
            partner = lax.dynamic_index_in_dim(plan[meeting], block, 0, keepdims=False)
            cols_x = lax.dynamic_index_in_dim(every_x, partner, 0, keepdims=False)
            cols_u = lax.dynamic_index_in_dim(every_u, partner, 0, keepdims=False)

            def add_sub(carry, index):
                start = (index * span).astype(jnp.int32)
                sub_x = lax.dynamic_slice_in_dim(cols_x, start, span, 0)
                sub_u = lax.dynamic_slice_in_dim(cols_u, start, span, 0)
                energy = kernel_tile(rows_x, sub_x)
                return carry + jnp.dot(energy, sub_u, preferred_element_type=jnp.float32), None

            total, unused = lax.scan(add_sub, total, jnp.arange(N_NARROW, dtype=jnp.int32))
        return (total * rows_a[:, None]).reshape(NB, P_SIZE, NPROBE).sum(axis=1)

    result = lax.map(one_group, jnp.arange(N_GROUP, dtype=jnp.int32))
    return result.reshape(NIMG, NPROBE)
```

```python
import functools

import jax
import jax.numpy as jnp
from jax import lax
from jax.experimental import pallas as pl
from jax.experimental.pallas import tpu as pltpu
from jax.sharding import PartitionSpec as P

P_SIZE = 49
PV = 75
NPROBE = 16
MEET = 4
IMGS = 16
GROUPS = 16
STEPS = 8
UNITS = 16
TILE = STEPS * UNITS
TILES = 7
DEPTH = 80
UROW = TILES * DEPTH
ROWS = UROW + 2 * NPROBE
SUBS = 10
LANES = 72
BLOCK = 2
RLIST = 32
FAR = -1.0e30
SCALE = 1.4426950408889634 / PV
MESH = pl.DeviceIdType.MESH
F32 = jnp.float32
BF16 = jnp.bfloat16
HALVES = ((0, 304), (304, 288))
VMEM = pl.BlockSpec(memory_space=pltpu.VMEM)
SMEM = pl.BlockSpec(memory_space=pltpu.SMEM)
ANY = pl.BlockSpec(memory_space=pl.ANY)


def two_parts(value):
    high = value.astype(BF16)
    return high, (value - high.astype(F32)).astype(BF16)


def pack_kernel(counts, weights, x_ref, probes_ref, item_ref, owner_ref):
    lane = lax.broadcasted_iota(jnp.int32, (1, TILES * TILE), 1)
    unit = lax.div(lane, TILE) * UNITS + lax.rem(lane, UNITS)
    step = lax.rem(lax.div(lane, UNITS), STEPS)
    whole = lax.broadcasted_iota(jnp.int32, (1, 128), 1)
    image, first, size = jnp.zeros_like(lane), jnp.zeros_like(lane), jnp.zeros_like(lane)
    owner = jnp.full_like(whole, -1)
    start = jnp.int32(0)
    for i in range(IMGS):
        count = counts[i]
        end = start + lax.div(count + (STEPS - 1), STEPS)
        inside = (unit >= start) & (unit < end)
        image = jnp.where(inside, i, image)
        first = jnp.where(inside, start, first)
        size = jnp.where(inside, count, size)
        owner = jnp.where((whole >= start) & (whole < end), i, owner)
        start = end
    patch = (unit - first) * STEPS + step
    valid = patch < size
    source = jnp.where(valid, image * P_SIZE + patch, -1)
    weight = jnp.ones(lane.shape, F32)
    for p in range(P_SIZE):
        weight = jnp.where(patch == p, weights[p], weight)
    alpha = weight / jnp.maximum(size, 1).astype(F32)
    rows = lax.broadcasted_iota(jnp.int32, (IMGS * P_SIZE, TILES * TILE), 0)
    pick = jnp.where(rows == source, 1.0, 0.0).astype(BF16)
    packed = lax.dot_general(
        x_ref[...], pick, (((0,), (0,)), ((), ())), preferred_element_type=F32
    )
    norm = jnp.sum(packed * packed, axis=0, keepdims=True)
    level = jnp.where(valid, PV * jnp.log(alpha) - 0.5 * norm, FAR)
    high = level.astype(BF16).astype(F32)
    low = level - high
    low = jnp.where(valid, low, 0.0)
    one = jnp.ones_like(level)
    full = jnp.concatenate([packed, high, low, one, one, jnp.zeros_like(one)], axis=0).astype(BF16)
    for t in range(TILES):
        item_ref[t * DEPTH : (t + 1) * DEPTH, :] = full[:, t * TILE : (t + 1) * TILE]
    tag = lax.broadcasted_iota(jnp.int32, (IMGS, 128), 0)
    mine = jnp.where(tag == owner, 1.0, 0.0).astype(BF16)
    owner_ref[...] = mine
    tiles = lax.div(start + (UNITS - 1), UNITS).astype(F32)
    lanes = lax.broadcasted_iota(jnp.int32, (NPROBE, 128), 1)
    for at, part in zip((UROW, UROW + NPROBE), two_parts(probes_ref[...])):
        spread = lax.dot_general(part, mine, (((0,), (0,)), ((), ())), preferred_element_type=F32)
        item_ref[at : at + NPROBE, :] = jnp.where(lanes >= 120, tiles, spread).astype(BF16)


def pack(x, counts, weights, probes):
    return pl.pallas_call(
        pack_kernel,
        out_shape=(
            jax.ShapeDtypeStruct((ROWS, 128), BF16),
            jax.ShapeDtypeStruct((IMGS, 128), BF16),
        ),
        in_specs=[SMEM, SMEM, VMEM, VMEM],
        out_specs=(VMEM, VMEM),
        name="pack",
    )(counts, weights, x, probes)


def places():
    g, n = lax.axis_index("group"), lax.axis_index("narrow")
    return g, n


def ring(n, by):
    return lax.div(n, 8) * 8 + lax.rem(lax.rem(n, 8) + by + 8, 8)


def along(g, by):
    return lax.div(g, 8) * 8 + lax.rem(lax.rem(g, 8) + 2 * by + 8, 8)


def flip(i):
    return lax.rem(i + 8, 16)


def sibling(g):
    return g + 1 - 2 * lax.rem(g, 2)


def gather_kernel(item, far, near, send_sem, recv_sem):
    g, n = places()
    up, down = ring(n, 1), ring(n, -1)
    right, left = along(g, 1), along(g, -1)
    over, twin = flip(g), sibling(g)
    peers = [(over, n), (right, n), (left, n), (twin, n), (g, up), (g, down), (over, flip(n))]
    barrier = pltpu.get_barrier_semaphore()
    for peer in peers:
        pl.semaphore_signal(barrier, inc=1, device_id=peer, device_id_type=MESH)
    pl.semaphore_wait(barrier, len(peers))

    def copy(which, half, src, dst, peer):
        at, size = HALVES[half]
        return pltpu.make_async_remote_copy(
            src_ref=src.at[pl.ds(at, size)],
            dst_ref=dst.at[pl.ds(at, size)],
            send_sem=send_sem.at[which, half],
            recv_sem=recv_sem.at[which, half],
            device_id=peer,
            device_id_type=MESH,
        )

    def across(which, owner, peer):
        return lambda half: copy(which, half, far.at[owner], far.at[owner], peer)

    def first(which, dst, peer):
        return lambda half: copy(which, half, item, dst, peer)

    plan = {
        "y": first(0, far.at[g], (over, n)),
        "right": first(1, far.at[g], (right, n)),
        "left": first(2, far.at[g], (left, n)),
        "up": first(3, near.at[1], (g, up)),
        "twin": first(4, far.at[g], (twin, n)),
        "yz": lambda half: copy(5, half, far.at[over], near.at[0], (over, flip(n))),
        "yright": across(6, over, (right, n)),
        "yleft": across(7, over, (left, n)),
        "right2": across(8, left, (right, n)),
        "yleft2": across(9, flip(right), (left, n)),
        "up2": lambda half: copy(10, half, near.at[1], near.at[2], (g, up)),
        "up3": lambda half: copy(11, half, near.at[2], near.at[3], (g, up)),
        "up4": lambda half: copy(12, half, near.at[3], near.at[4], (g, up)),
        "down": lambda half: copy(13, half, near.at[0], near.at[5], (g, down)),
        "down2": lambda half: copy(14, half, near.at[5], near.at[6], (g, down)),
        "down3": lambda half: copy(15, half, near.at[6], near.at[7], (g, down)),
        "down4": lambda half: copy(16, half, near.at[7], near.at[8], (g, down)),
        "ty": across(17, over, (twin, n)),
        "tleft": across(18, left, (twin, n)),
        "tright": across(19, right, (twin, n)),
        "tyleft": across(20, flip(left), (twin, n)),
        "tyright": across(21, flip(right), (twin, n)),
        "tfar": across(22, along(g, 2), (twin, n)),
        "tyfar": across(23, flip(along(g, 2)), (twin, n)),
    }
    for half in range(2):
        for name in ("y", "up", "right", "left", "twin"):
            plan[name](half).start()
    arrivals = [
        [("y", ("yz", "yright", "yleft", "ty")), ("up", ("up2",)), ("right", ("right2", "tleft")), ("left", ("tright",))],
        [("yz", ("down",)), ("up2", ("up3",)), ("yleft", ("yleft2", "tyright")), ("yright", ("tyleft",))],
        [("up3", ("up4",)), ("down", ("down2",)), ("right2", ("tfar",)), ("yleft2", ("tyfar",))],
        [("down2", ("down3",)), ("down3", ("down4",)), ("up4", ()), ("down4", ())],
    ]
    for wave in arrivals:
        for half in range(2):
            for name, onward in wave:
                plan[name](half).wait_recv()
                for other in onward:
                    plan[other](half).start()
    for half in range(2):
        for name in ("twin", "ty", "tleft", "tright", "tyleft", "tyright", "tfar", "tyfar"):
            plan[name](half).wait_recv()
    for half in range(2):
        for name in plan:
            plan[name](half).wait_send()


def gather(item):
    return pl.pallas_call(
        gather_kernel,
        out_shape=(
            jax.ShapeDtypeStruct((GROUPS, ROWS, 128), BF16),
            jax.ShapeDtypeStruct((9, ROWS, 128), BF16),
        ),
        in_specs=[ANY],
        out_specs=(ANY, ANY),
        scratch_shapes=[pltpu.SemaphoreType.DMA((24, 2)), pltpu.SemaphoreType.DMA((24, 2))],
        compiler_params=pltpu.CompilerParams(collective_id=0, has_side_effects=True),
        name="gather",
    )(item)


def tile_count(block):
    lanes = lax.broadcasted_iota(jnp.int32, block.shape, 1)
    return jnp.max(jnp.where(lanes >= 120, block.astype(F32), 0.0)).astype(jnp.int32)


def meet_kernel(
    plan, item, near, far, near_out, far_out,
    subs, parts, cols, col_u, rows, row_u, q_list, p_list, p_whole, q_whole, sems,
):
    g = lax.axis_index("group")
    partner = [plan[m, g] for m in range(MEET)]
    order = [item, near.at[0], near.at[1], near.at[2], near.at[3], near.at[5], near.at[6], near.at[7], near.at[4], near.at[8]]
    loads = [pltpu.make_async_copy(src, subs.at[r], sems.at[r]) for r, src in enumerate(order)]
    loads += [
        pltpu.make_async_copy(far.at[partner[m]], parts.at[m], sems.at[SUBS + m]) for m in range(MEET)
    ]
    for load in loads:
        load.start()
    q_list[...] = jnp.zeros_like(q_list)
    p_list[...] = jnp.zeros_like(p_list)
    p_whole[...] = jnp.zeros_like(p_whole)
    q_whole[...] = jnp.zeros_like(q_whole)
    far_out[...] = jnp.zeros_like(far_out)
    depth = lax.broadcasted_iota(jnp.int32, (DEPTH, TILE), 0)
    empty_cols = jnp.where(depth == PV, FAR, 0.0).astype(BF16)
    lane = lax.broadcasted_iota(jnp.int32, (TILE, DEPTH), 1)
    empty_rows = jnp.where(lane == PV + 2, FAR, 0.0).astype(BF16)
    a = lax.broadcasted_iota(jnp.int32, (DEPTH, DEPTH), 0)
    b = lax.broadcasted_iota(jnp.int32, (DEPTH, DEPTH), 1)
    moved = jnp.where(a < PV, a, jnp.where(a < PV + 2, a + 2, jnp.where(a < PV + 4, a - 2, a)))
    swap = jnp.where(moved == b, 1.0, 0.0).astype(BF16)
    for load in loads:
        load.wait()

    def spread_units(block):
        return jnp.transpose(block.astype(F32), (1, 0)).astype(BF16)

    at = jnp.int32(0)
    col_at, col_tiles, edges = [], [], [at]
    for r in range(SUBS):
        tiles = tile_count(subs[r, UROW : UROW + NPROBE, :])
        units = spread_units(subs[r, UROW:ROWS, :])
        for t in range(TILES):

            @pl.when(t < tiles)
            def _():
                cols[at + t] = subs[r, t * DEPTH : (t + 1) * DEPTH, :]
                col_u[at + t] = jnp.concatenate([units[t * UNITS : (t + 1) * UNITS]] * STEPS, axis=0)

        col_at.append(at)
        col_tiles.append(tiles)
        at = at + tiles
        if r in (1, 7, 9):
            cols[at] = empty_cols
            col_u[at] = jnp.zeros((TILE, 2 * NPROBE), BF16)
            at = lax.div(at + 1, 2) * 2
            edges.append(lax.div(at, 2))

    row_tiles = [tile_count(parts[m, UROW : UROW + NPROBE, :]) for m in range(MEET)]
    later = [partner[m] > g for m in range(MEET)]
    row_at = [jnp.int32(0)] * MEET
    at = jnp.int32(0)
    middle = at
    for side in range(2):
        for m in range(MEET):
            here = later[m] if side == 0 else jnp.logical_not(later[m])
            row_at[m] = jnp.where(here, at, row_at[m])
            at = at + jnp.where(here, row_tiles[m], 0)
        for extra in range(BLOCK - 1):
            rows[at + extra] = empty_rows
            row_u[at + extra] = jnp.zeros((UNITS, 2 * NPROBE), BF16)
        at = lax.div(at + BLOCK - 1, BLOCK) * BLOCK
        if side == 0:
            middle = lax.div(at, BLOCK)
    last = lax.div(at, BLOCK)
    for m in range(MEET):
        units = spread_units(parts[m, UROW:ROWS, :])
        for t in range(TILES):

            @pl.when(t < row_tiles[m])
            def _():
                turned = lax.dot_general(
                    parts[m, t * DEPTH : (t + 1) * DEPTH, :], swap,
                    (((0,), (0,)), ((), ())), preferred_element_type=F32,
                )
                rows[row_at[m] + t] = turned.astype(BF16)
                row_u[row_at[m] + t] = units[t * UNITS : (t + 1) * UNITS]

    def job(first_pair, last_pair, first_block, last_block):
        def pair_body(pair, carry):
            right = jnp.concatenate([cols[2 * pair], cols[2 * pair + 1]], axis=1)
            right_u = jnp.concatenate([col_u[2 * pair], col_u[2 * pair + 1]], axis=0)

            def block_body(block, total):
                left = rows[pl.ds(block * BLOCK, BLOCK)].reshape(BLOCK * TILE, DEPTH)
                left_u = row_u[pl.ds(block * BLOCK, BLOCK)].reshape(BLOCK * UNITS, 2 * NPROBE)
                inner = jnp.dot(left, right, preferred_element_type=F32)
                energy = jnp.exp2(inner * SCALE)
                sums = energy.reshape(BLOCK, STEPS, UNITS, 2 * TILE).sum(axis=1)
                sums = sums.reshape(BLOCK * UNITS, 2 * TILE).astype(BF16)
                q = jnp.dot(sums, right_u, preferred_element_type=F32)
                q_list[pl.ds(block * BLOCK, BLOCK)] += q.reshape(BLOCK, UNITS, 2 * NPROBE)
                return total + lax.dot_general(
                    left_u, sums, (((0,), (0,)), ((), ())), preferred_element_type=F32
                )

            total = lax.fori_loop(
                first_block, last_block, block_body, jnp.zeros((2 * NPROBE, 2 * TILE), F32)
            )
            p_list[2 * pair] += total[:, :TILE]
            p_list[2 * pair + 1] += total[:, TILE:]
            return carry

        lax.fori_loop(first_pair, last_pair, pair_body, 0)

    job(edges[0], edges[1], 0, middle)
    job(edges[1], edges[2], 0, last)
    job(edges[2], edges[3], middle, last)

    for r in range(SUBS):
        for t in range(TILES):

            @pl.when(t < col_tiles[r])
            def _():
                both = p_list[col_at[r] + t]
                high, low = two_parts(both[:NPROBE] + both[NPROBE:])
                p_whole[2 * r * NPROBE : (2 * r + 1) * NPROBE, t * TILE : (t + 1) * TILE] = high
                p_whole[(2 * r + 1) * NPROBE : (2 * r + 2) * NPROBE, t * TILE : (t + 1) * TILE] = low

    a = lax.broadcasted_iota(jnp.int32, (TILES * TILE, 128), 0)
    b = lax.broadcasted_iota(jnp.int32, (TILES * TILE, 128), 1)
    gather_units = jnp.where(lax.div(a, TILE) * UNITS + lax.rem(a, UNITS) == b, 1.0, 0.0).astype(BF16)
    units = jnp.dot(p_whole[...], gather_units, preferred_element_type=F32)
    for r in range(SUBS):
        near_out[r] = (
            units[2 * r * NPROBE : (2 * r + 1) * NPROBE]
            + units[(2 * r + 1) * NPROBE : (2 * r + 2) * NPROBE]
        )
    for m in range(MEET):
        for t in range(TILES):

            @pl.when(t < row_tiles[m])
            def _():
                q_whole[m, t * UNITS : (t + 1) * UNITS, : 2 * NPROBE] = q_list[row_at[m] + t]

        turned = jnp.transpose(q_whole[m], (1, 0))
        far_out[partner[m]] += turned[:NPROBE] + turned[NPROBE : 2 * NPROBE]


def meet(plan, item, near, far):
    return pl.pallas_call(
        meet_kernel,
        out_shape=(
            jax.ShapeDtypeStruct((SUBS, NPROBE, 128), F32),
            jax.ShapeDtypeStruct((GROUPS, NPROBE, 128), F32),
        ),
        in_specs=[SMEM, ANY, ANY, ANY],
        out_specs=(VMEM, VMEM),
        scratch_shapes=[
            pltpu.VMEM((SUBS, ROWS, 128), BF16),
            pltpu.VMEM((MEET, ROWS, 128), BF16),
            pltpu.VMEM((LANES, DEPTH, TILE), BF16),
            pltpu.VMEM((LANES, TILE, 2 * NPROBE), BF16),
            pltpu.VMEM((RLIST, TILE, DEPTH), BF16),
            pltpu.VMEM((RLIST, UNITS, 2 * NPROBE), BF16),
            pltpu.VMEM((RLIST, UNITS, 2 * NPROBE), F32),
            pltpu.VMEM((LANES, 2 * NPROBE, TILE), F32),
            pltpu.VMEM((SUBS * 2 * NPROBE, TILES * TILE), BF16),
            pltpu.VMEM((MEET, 128, 128), F32),
            pltpu.SemaphoreType.DMA((SUBS + MEET,)),
        ],
        name="meet",
    )(plan, item, near, far)


def home_kernel(near_part, far_part, owner, out, from_near, from_far, near_send, near_recv, far_send, far_recv):
    g, n = places()
    barrier = pltpu.get_barrier_semaphore()
    for k in range(1, 16):
        pl.semaphore_signal(barrier, inc=1, device_id=(g, lax.rem(n + k, 16)), device_id_type=MESH)
        pl.semaphore_signal(barrier, inc=1, device_id=(lax.rem(g + k, 16), n), device_id_type=MESH)
    pl.semaphore_wait(barrier, 30)
    across = flip(n)
    targets = [across, ring(n, -1), ring(n, -2), ring(n, -3), ring(across, 1), ring(across, 2), ring(across, 3), ring(n, -4), ring(across, 4)]
    copies = []
    for j, target in enumerate(targets):
        copies.append(
            pltpu.make_async_remote_copy(
                src_ref=near_part.at[j + 1], dst_ref=from_near.at[j],
                send_sem=near_send.at[j], recv_sem=near_recv.at[j],
                device_id=(g, target), device_id_type=MESH,
            )
        )
    for k in range(1, 16):
        target = lax.rem(g + k, 16)
        copies.append(
            pltpu.make_async_remote_copy(
                src_ref=far_part.at[target], dst_ref=from_far.at[k - 1],
                send_sem=far_send.at[k - 1], recv_sem=far_recv.at[k - 1],
                device_id=(target, n), device_id_type=MESH,
            )
        )
    for one in copies:
        one.start()
    for one in copies:
        one.wait_recv()
    total = near_part[0]
    for j in range(9):
        total = total + from_near[j]
    for k in range(15):
        total = total + from_far[k]
    result = jnp.zeros((IMGS, NPROBE), F32)
    rest = total
    for part in range(3):
        piece = rest.astype(BF16)
        rest = rest - piece.astype(F32)
        result = result + lax.dot_general(
            owner[...], piece, (((1,), (1,)), ((), ())), preferred_element_type=F32
        )
    out[...] = result
    for one in copies:
        one.wait_send()


def home(near_part, far_part, owner):
    return pl.pallas_call(
        home_kernel,
        out_shape=jax.ShapeDtypeStruct((IMGS, NPROBE), F32),
        in_specs=[VMEM, VMEM, VMEM],
        out_specs=VMEM,
        scratch_shapes=[
            pltpu.VMEM((9, NPROBE, 128), F32),
            pltpu.VMEM((15, NPROBE, 128), F32),
            pltpu.SemaphoreType.DMA((9,)),
            pltpu.SemaphoreType.DMA((9,)),
            pltpu.SemaphoreType.DMA((15,)),
            pltpu.SemaphoreType.DMA((15,)),
        ],
        compiler_params=pltpu.CompilerParams(collective_id=1, has_side_effects=True),
        name="home",
    )(near_part, far_part, owner)


def shards(patches, counts, weights, probes, plan):
    item, owner = pack(patches.reshape(IMGS * P_SIZE, PV), counts, weights, probes)
    far, near = gather(item)
    near_part, far_part = meet(plan, item, near, far)
    return home(near_part, far_part, owner)


def solution(mesh):
    return jax.shard_map(
        shards,
        mesh=mesh,
        in_specs=(
            P(("group", "narrow"), None),
            P(("group", "narrow")),
            P(),
            P(("group", "narrow"), None),
            P(),
        ),
        out_specs=P(("group", "narrow"), None),
        check_vma=False,
    )
```

```python
import functools

import jax
import jax.numpy as jnp
from jax import lax
from jax.experimental import pallas as pl
from jax.experimental.pallas import tpu as pltpu
from jax.sharding import PartitionSpec as P

P_SIZE = 49
PV = 75
NPROBE = 16
MEET = 4
IMGS = 16
GROUPS = 16
STEPS = 8
UNITS = 16
TILE = STEPS * UNITS
TILES = 7
DEPTH = 80
UROW = TILES * DEPTH
ROWS = UROW + 2 * NPROBE
SUBS = 10
LANES = 72
BLOCK = 4
RLIST = 40
FAR = -1.0e30
SCALE = 1.4426950408889634 / PV
MESH = pl.DeviceIdType.MESH
F32 = jnp.float32
BF16 = jnp.bfloat16
HALVES = ((0, 304), (304, 288))
VMEM = pl.BlockSpec(memory_space=pltpu.VMEM)
SMEM = pl.BlockSpec(memory_space=pltpu.SMEM)
ANY = pl.BlockSpec(memory_space=pl.ANY)


def two_parts(value):
    high = value.astype(BF16)
    return high, (value - high.astype(F32)).astype(BF16)


def pack_kernel(counts, weights, x_ref, probes_ref, item_ref, owner_ref):
    lane = lax.broadcasted_iota(jnp.int32, (1, TILES * TILE), 1)
    unit = lax.div(lane, TILE) * UNITS + lax.rem(lane, UNITS)
    step = lax.rem(lax.div(lane, UNITS), STEPS)
    whole = lax.broadcasted_iota(jnp.int32, (1, 128), 1)
    image, first, size = jnp.zeros_like(lane), jnp.zeros_like(lane), jnp.zeros_like(lane)
    owner = jnp.full_like(whole, -1)
    start = jnp.int32(0)
    for i in range(IMGS):
        count = counts[i]
        end = start + lax.div(count + (STEPS - 1), STEPS)
        inside = (unit >= start) & (unit < end)
        image = jnp.where(inside, i, image)
        first = jnp.where(inside, start, first)
        size = jnp.where(inside, count, size)
        owner = jnp.where((whole >= start) & (whole < end), i, owner)
        start = end
    patch = (unit - first) * STEPS + step
    valid = patch < size
    source = jnp.where(valid, image * P_SIZE + patch, -1)
    weight = jnp.ones(lane.shape, F32)
    for p in range(P_SIZE):
        weight = jnp.where(patch == p, weights[p], weight)
    alpha = weight / jnp.maximum(size, 1).astype(F32)
    rows = lax.broadcasted_iota(jnp.int32, (IMGS * P_SIZE, TILES * TILE), 0)
    pick = jnp.where(rows == source, 1.0, 0.0).astype(BF16)
    packed = lax.dot_general(
        x_ref[...], pick, (((0,), (0,)), ((), ())), preferred_element_type=F32
    )
    norm = jnp.sum(packed * packed, axis=0, keepdims=True)
    level = jnp.where(valid, PV * jnp.log(alpha) - 0.5 * norm, FAR)
    high = level.astype(BF16).astype(F32)
    low = level - high
    low = jnp.where(valid, low, 0.0)
    one = jnp.ones_like(level)
    full = jnp.concatenate([packed, high, low, one, one, jnp.zeros_like(one)], axis=0).astype(BF16)
    for t in range(TILES):
        item_ref[t * DEPTH : (t + 1) * DEPTH, :] = full[:, t * TILE : (t + 1) * TILE]
    tag = lax.broadcasted_iota(jnp.int32, (IMGS, 128), 0)
    mine = jnp.where(tag == owner, 1.0, 0.0).astype(BF16)
    owner_ref[...] = mine
    tiles = lax.div(start + (UNITS - 1), UNITS).astype(F32)
    lanes = lax.broadcasted_iota(jnp.int32, (NPROBE, 128), 1)
    for at, part in zip((UROW, UROW + NPROBE), two_parts(probes_ref[...])):
        spread = lax.dot_general(part, mine, (((0,), (0,)), ((), ())), preferred_element_type=F32)
        item_ref[at : at + NPROBE, :] = jnp.where(lanes >= 120, tiles, spread).astype(BF16)


def pack(x, counts, weights, probes):
    return pl.pallas_call(
        pack_kernel,
        out_shape=(
            jax.ShapeDtypeStruct((ROWS, 128), BF16),
            jax.ShapeDtypeStruct((IMGS, 128), BF16),
        ),
        in_specs=[SMEM, SMEM, VMEM, VMEM],
        out_specs=(VMEM, VMEM),
        name="pack",
    )(counts, weights, x, probes)


def places():
    g, n = lax.axis_index("group"), lax.axis_index("narrow")
    return g, n


def ring(n, by):
    return lax.div(n, 8) * 8 + lax.rem(lax.rem(n, 8) + by + 8, 8)


def along(g, by):
    return lax.div(g, 8) * 8 + lax.rem(lax.rem(g, 8) + 2 * by + 8, 8)


def flip(i):
    return lax.rem(i + 8, 16)


def sibling(g):
    return g + 1 - 2 * lax.rem(g, 2)


def gather_kernel(item, far, near, send_sem, recv_sem):
    g, n = places()
    up, down = ring(n, 1), ring(n, -1)
    right, left = along(g, 1), along(g, -1)
    over, twin = flip(g), sibling(g)
    peers = [(over, n), (right, n), (left, n), (twin, n), (g, up), (g, down), (over, flip(n))]
    barrier = pltpu.get_barrier_semaphore()
    for peer in peers:
        pl.semaphore_signal(barrier, inc=1, device_id=peer, device_id_type=MESH)
    pl.semaphore_wait(barrier, len(peers))

    def copy(which, half, src, dst, peer):
        at, size = HALVES[half]
        return pltpu.make_async_remote_copy(
            src_ref=src.at[pl.ds(at, size)],
            dst_ref=dst.at[pl.ds(at, size)],
            send_sem=send_sem.at[which, half],
            recv_sem=recv_sem.at[which, half],
            device_id=peer,
            device_id_type=MESH,
        )

    def across(which, owner, peer):
        return lambda half: copy(which, half, far.at[owner], far.at[owner], peer)

    def first(which, dst, peer):
        return lambda half: copy(which, half, item, dst, peer)

    plan = {
        "y": first(0, far.at[g], (over, n)),
        "right": first(1, far.at[g], (right, n)),
        "left": first(2, far.at[g], (left, n)),
        "up": first(3, near.at[1], (g, up)),
        "twin": first(4, far.at[g], (twin, n)),
        "yz": lambda half: copy(5, half, far.at[over], near.at[0], (over, flip(n))),
        "yright": across(6, over, (right, n)),
        "yleft": across(7, over, (left, n)),
        "right2": across(8, left, (right, n)),
        "yleft2": across(9, flip(right), (left, n)),
        "up2": lambda half: copy(10, half, near.at[1], near.at[2], (g, up)),
        "up3": lambda half: copy(11, half, near.at[2], near.at[3], (g, up)),
        "up4": lambda half: copy(12, half, near.at[3], near.at[4], (g, up)),
        "down": lambda half: copy(13, half, near.at[0], near.at[5], (g, down)),
        "down2": lambda half: copy(14, half, near.at[5], near.at[6], (g, down)),
        "down3": lambda half: copy(15, half, near.at[6], near.at[7], (g, down)),
        "down4": lambda half: copy(16, half, near.at[7], near.at[8], (g, down)),
        "ty": across(17, over, (twin, n)),
        "tleft": across(18, left, (twin, n)),
        "tright": across(19, right, (twin, n)),
        "tyleft": across(20, flip(left), (twin, n)),
        "tyright": across(21, flip(right), (twin, n)),
        "tfar": across(22, along(g, 2), (twin, n)),
        "tyfar": across(23, flip(along(g, 2)), (twin, n)),
    }
    for half in range(2):
        for name in ("y", "up", "right", "left", "twin"):
            plan[name](half).start()
    arrivals = [
        [("y", ("yz", "yright", "yleft", "ty")), ("up", ("up2",)), ("right", ("right2", "tleft")), ("left", ("tright",))],
        [("yz", ("down",)), ("up2", ("up3",)), ("yleft", ("yleft2", "tyright")), ("yright", ("tyleft",))],
        [("up3", ("up4",)), ("down", ("down2",)), ("right2", ("tfar",)), ("yleft2", ("tyfar",))],
        [("down2", ("down3",)), ("down3", ("down4",)), ("up4", ()), ("down4", ())],
    ]
    for wave in arrivals:
        for half in range(2):
            for name, onward in wave:
                plan[name](half).wait_recv()
                for other in onward:
                    plan[other](half).start()
    for half in range(2):
        for name in ("twin", "ty", "tleft", "tright", "tyleft", "tyright", "tfar", "tyfar"):
            plan[name](half).wait_recv()
    for half in range(2):
        for name in plan:
            plan[name](half).wait_send()


def gather(item):
    return pl.pallas_call(
        gather_kernel,
        out_shape=(
            jax.ShapeDtypeStruct((GROUPS, ROWS, 128), BF16),
            jax.ShapeDtypeStruct((9, ROWS, 128), BF16),
        ),
        in_specs=[ANY],
        out_specs=(ANY, ANY),
        scratch_shapes=[pltpu.SemaphoreType.DMA((24, 2)), pltpu.SemaphoreType.DMA((24, 2))],
        compiler_params=pltpu.CompilerParams(collective_id=0, has_side_effects=True),
        name="gather",
    )(item)


def tile_count(block):
    lanes = lax.broadcasted_iota(jnp.int32, block.shape, 1)
    return jnp.max(jnp.where(lanes >= 120, block.astype(F32), 0.0)).astype(jnp.int32)


def meet_kernel(
    plan, item, near, far, near_out, far_out,
    subs, parts, cols, col_u, rows, row_u, q_list, p_list, p_whole, q_whole, sems,
):
    g = lax.axis_index("group")
    partner = [plan[m, g] for m in range(MEET)]
    order = [item, near.at[0], near.at[1], near.at[2], near.at[3], near.at[5], near.at[6], near.at[7], near.at[4], near.at[8]]
    loads = [pltpu.make_async_copy(src, subs.at[r], sems.at[r]) for r, src in enumerate(order)]
    loads += [
        pltpu.make_async_copy(far.at[partner[m]], parts.at[m], sems.at[SUBS + m]) for m in range(MEET)
    ]
    for load in loads:
        load.start()
    q_list[...] = jnp.zeros_like(q_list)
    p_list[...] = jnp.zeros_like(p_list)
    p_whole[...] = jnp.zeros_like(p_whole)
    q_whole[...] = jnp.zeros_like(q_whole)
    far_out[...] = jnp.zeros_like(far_out)
    depth = lax.broadcasted_iota(jnp.int32, (DEPTH, TILE), 0)
    empty_cols = jnp.where(depth == PV, FAR, 0.0).astype(BF16)
    lane = lax.broadcasted_iota(jnp.int32, (TILE, DEPTH), 1)
    empty_rows = jnp.where(lane == PV + 2, FAR, 0.0).astype(BF16)
    a = lax.broadcasted_iota(jnp.int32, (DEPTH, DEPTH), 0)
    b = lax.broadcasted_iota(jnp.int32, (DEPTH, DEPTH), 1)
    moved = jnp.where(a < PV, a, jnp.where(a < PV + 2, a + 2, jnp.where(a < PV + 4, a - 2, a)))
    swap = jnp.where(moved == b, 1.0, 0.0).astype(BF16)
    for load in loads:
        load.wait()

    def spread_units(block):
        return jnp.transpose(block.astype(F32), (1, 0)).astype(BF16)

    at = jnp.int32(0)
    col_at, col_tiles, edges = [], [], [at]
    for r in range(SUBS):
        tiles = tile_count(subs[r, UROW : UROW + NPROBE, :])
        units = spread_units(subs[r, UROW:ROWS, :])
        for t in range(TILES):

            @pl.when(t < tiles)
            def _():
                cols[at + t] = subs[r, t * DEPTH : (t + 1) * DEPTH, :]
                col_u[at + t] = jnp.concatenate([units[t * UNITS : (t + 1) * UNITS]] * STEPS, axis=0)

        col_at.append(at)
        col_tiles.append(tiles)
        at = at + tiles
        if r in (1, 7, 9):
            cols[at] = empty_cols
            col_u[at] = jnp.zeros((TILE, 2 * NPROBE), BF16)
            at = lax.div(at + 1, 2) * 2
            edges.append(lax.div(at, 2))

    row_tiles = [tile_count(parts[m, UROW : UROW + NPROBE, :]) for m in range(MEET)]
    later = [partner[m] > g for m in range(MEET)]
    row_at = [jnp.int32(0)] * MEET
    at = jnp.int32(0)
    middle = at
    for side in range(2):
        for m in range(MEET):
            here = later[m] if side == 0 else jnp.logical_not(later[m])
            row_at[m] = jnp.where(here, at, row_at[m])
            at = at + jnp.where(here, row_tiles[m], 0)
        for extra in range(BLOCK - 1):
            rows[at + extra] = empty_rows
            row_u[at + extra] = jnp.zeros((UNITS, 2 * NPROBE), BF16)
        at = lax.div(at + BLOCK - 1, BLOCK) * BLOCK
        if side == 0:
            middle = lax.div(at, BLOCK)
    last = lax.div(at, BLOCK)
    for m in range(MEET):
        units = spread_units(parts[m, UROW:ROWS, :])
        for t in range(TILES):

            @pl.when(t < row_tiles[m])
            def _():
                turned = lax.dot_general(
                    parts[m, t * DEPTH : (t + 1) * DEPTH, :], swap,
                    (((0,), (0,)), ((), ())), preferred_element_type=F32,
                )
                rows[row_at[m] + t] = turned.astype(BF16)
                row_u[row_at[m] + t] = units[t * UNITS : (t + 1) * UNITS]

    def job(first_pair, last_pair, first_block, last_block):
        def pair_body(pair, carry):
            right = jnp.concatenate([cols[2 * pair], cols[2 * pair + 1]], axis=1)
            right_u = jnp.concatenate([col_u[2 * pair], col_u[2 * pair + 1]], axis=0)

            def block_body(block, total):
                left = rows[pl.ds(block * BLOCK, BLOCK)].reshape(BLOCK * TILE, DEPTH)
                left_u = row_u[pl.ds(block * BLOCK, BLOCK)].reshape(BLOCK * UNITS, 2 * NPROBE)
                inner = jnp.dot(left, right, preferred_element_type=F32)
                energy = jnp.exp2(inner * SCALE)
                sums = energy.reshape(BLOCK, STEPS, UNITS, 2 * TILE).sum(axis=1)
                sums = sums.reshape(BLOCK * UNITS, 2 * TILE).astype(BF16)
                q = jnp.dot(sums, right_u, preferred_element_type=F32)
                q_list[pl.ds(block * BLOCK, BLOCK)] += q.reshape(BLOCK, UNITS, 2 * NPROBE)
                return total + lax.dot_general(
                    left_u, sums, (((0,), (0,)), ((), ())), preferred_element_type=F32
                )

            total = lax.fori_loop(
                first_block, last_block, block_body, jnp.zeros((2 * NPROBE, 2 * TILE), F32)
            )
            p_list[2 * pair] += total[:, :TILE]
            p_list[2 * pair + 1] += total[:, TILE:]
            return carry

        lax.fori_loop(first_pair, last_pair, pair_body, 0)

    job(edges[0], edges[1], 0, middle)
    job(edges[1], edges[2], 0, last)
    job(edges[2], edges[3], middle, last)

    for r in range(SUBS):
        for t in range(TILES):

            @pl.when(t < col_tiles[r])
            def _():
                both = p_list[col_at[r] + t]
                high, low = two_parts(both[:NPROBE] + both[NPROBE:])
                p_whole[2 * r * NPROBE : (2 * r + 1) * NPROBE, t * TILE : (t + 1) * TILE] = high
                p_whole[(2 * r + 1) * NPROBE : (2 * r + 2) * NPROBE, t * TILE : (t + 1) * TILE] = low

    a = lax.broadcasted_iota(jnp.int32, (TILES * TILE, 128), 0)
    b = lax.broadcasted_iota(jnp.int32, (TILES * TILE, 128), 1)
    gather_units = jnp.where(lax.div(a, TILE) * UNITS + lax.rem(a, UNITS) == b, 1.0, 0.0).astype(BF16)
    units = jnp.dot(p_whole[...], gather_units, preferred_element_type=F32)
    for r in range(SUBS):
        near_out[r] = (
            units[2 * r * NPROBE : (2 * r + 1) * NPROBE]
            + units[(2 * r + 1) * NPROBE : (2 * r + 2) * NPROBE]
        )
    for m in range(MEET):
        for t in range(TILES):

            @pl.when(t < row_tiles[m])
            def _():
                q_whole[m, t * UNITS : (t + 1) * UNITS, : 2 * NPROBE] = q_list[row_at[m] + t]

        turned = jnp.transpose(q_whole[m], (1, 0))
        far_out[partner[m]] += turned[:NPROBE] + turned[NPROBE : 2 * NPROBE]


def meet(plan, item, near, far):
    return pl.pallas_call(
        meet_kernel,
        out_shape=(
            jax.ShapeDtypeStruct((SUBS, NPROBE, 128), F32),
            jax.ShapeDtypeStruct((GROUPS, NPROBE, 128), F32),
        ),
        in_specs=[SMEM, ANY, ANY, ANY],
        out_specs=(VMEM, VMEM),
        scratch_shapes=[
            pltpu.VMEM((SUBS, ROWS, 128), BF16),
            pltpu.VMEM((MEET, ROWS, 128), BF16),
            pltpu.VMEM((LANES, DEPTH, TILE), BF16),
            pltpu.VMEM((LANES, TILE, 2 * NPROBE), BF16),
            pltpu.VMEM((RLIST, TILE, DEPTH), BF16),
            pltpu.VMEM((RLIST, UNITS, 2 * NPROBE), BF16),
            pltpu.VMEM((RLIST, UNITS, 2 * NPROBE), F32),
            pltpu.VMEM((LANES, 2 * NPROBE, TILE), F32),
            pltpu.VMEM((SUBS * 2 * NPROBE, TILES * TILE), BF16),
            pltpu.VMEM((MEET, 128, 128), F32),
            pltpu.SemaphoreType.DMA((SUBS + MEET,)),
        ],
        name="meet",
    )(plan, item, near, far)


def home_kernel(near_part, far_part, owner, out, from_near, from_far, near_send, near_recv, far_send, far_recv):
    g, n = places()
    barrier = pltpu.get_barrier_semaphore()
    for k in range(1, 16):
        pl.semaphore_signal(barrier, inc=1, device_id=(g, lax.rem(n + k, 16)), device_id_type=MESH)
        pl.semaphore_signal(barrier, inc=1, device_id=(lax.rem(g + k, 16), n), device_id_type=MESH)
    pl.semaphore_wait(barrier, 30)
    across = flip(n)
    targets = [across, ring(n, -1), ring(n, -2), ring(n, -3), ring(across, 1), ring(across, 2), ring(across, 3), ring(n, -4), ring(across, 4)]
    copies = []
    for j, target in enumerate(targets):
        copies.append(
            pltpu.make_async_remote_copy(
                src_ref=near_part.at[j + 1], dst_ref=from_near.at[j],
                send_sem=near_send.at[j], recv_sem=near_recv.at[j],
                device_id=(g, target), device_id_type=MESH,
            )
        )
    for k in range(1, 16):
        target = lax.rem(g + k, 16)
        copies.append(
            pltpu.make_async_remote_copy(
                src_ref=far_part.at[target], dst_ref=from_far.at[k - 1],
                send_sem=far_send.at[k - 1], recv_sem=far_recv.at[k - 1],
                device_id=(target, n), device_id_type=MESH,
            )
        )
    for one in copies:
        one.start()
    for one in copies:
        one.wait_recv()
    total = near_part[0]
    for j in range(9):
        total = total + from_near[j]
    for k in range(15):
        total = total + from_far[k]
    result = jnp.zeros((IMGS, NPROBE), F32)
    rest = total
    for part in range(3):
        piece = rest.astype(BF16)
        rest = rest - piece.astype(F32)
        result = result + lax.dot_general(
            owner[...], piece, (((1,), (1,)), ((), ())), preferred_element_type=F32
        )
    out[...] = result
    for one in copies:
        one.wait_send()


def home(near_part, far_part, owner):
    return pl.pallas_call(
        home_kernel,
        out_shape=jax.ShapeDtypeStruct((IMGS, NPROBE), F32),
        in_specs=[VMEM, VMEM, VMEM],
        out_specs=VMEM,
        scratch_shapes=[
            pltpu.VMEM((9, NPROBE, 128), F32),
            pltpu.VMEM((15, NPROBE, 128), F32),
            pltpu.SemaphoreType.DMA((9,)),
            pltpu.SemaphoreType.DMA((9,)),
            pltpu.SemaphoreType.DMA((15,)),
            pltpu.SemaphoreType.DMA((15,)),
        ],
        compiler_params=pltpu.CompilerParams(collective_id=1, has_side_effects=True),
        name="home",
    )(near_part, far_part, owner)


def shards(patches, counts, weights, probes, plan):
    item, owner = pack(patches.reshape(IMGS * P_SIZE, PV), counts, weights, probes)
    far, near = gather(item)
    near_part, far_part = meet(plan, item, near, far)
    return home(near_part, far_part, owner)


def solution(mesh):
    return jax.shard_map(
        shards,
        mesh=mesh,
        in_specs=(
            P(("group", "narrow"), None),
            P(("group", "narrow")),
            P(),
            P(("group", "narrow"), None),
            P(),
        ),
        out_specs=P(("group", "narrow"), None),
        check_vma=False,
    )
```
